32 devices in a mesh: patch: 2 (over x), row: 4 (over y, core), col: 4 (over z).
Axes of the slice: x: 2, y: 2, z: 4, core: 2. Of those that a mesh axis runs over, the one named last changes fastest.
Arguments:
- sky_cube: float32 [512, 128, 512], P(None, ('patch', 'row'), 'col'), parts along dimension 1, may hold values from -40 to 140
- beam_taps: float32 [512, 33], replicated, may hold values from 0 to 0.2
Outputs:
- cleaned_cube: float32 [512, 128, 512], P(None, ('patch', 'row'), 'col'), parts along dimension 1
The draws below stay inside these ranges and needn't reach their ends.
There are 2 independent parts, one for each index of `patch`. The reference program is written for one: setup_inputs(seed, part) draws one part's arguments, and reference() takes and returns one part's arrays. A program takes and returns all parts, laid end to end along the dimension named above; an argument that names none is the same for every part. Nothing has to cross between parts.
All inputs are finite; a program needn't handle non-finite values.
Results may differ from the reference program's by a relative error of at most 0.00085.
Values sent between devices are 32-bit elements; how exact they have to be, the bound alone decides.
No kernel may reach another device: no remote copies, remote signals or barrier semaphores. Data moves between devices by JAX's collectives and lax.ppermute only.
A program may use at most 64 MiB of HBM per device.

```python
import jax
import jax.numpy as jnp
from jax import lax

CHANNELS = 512
TAPS = 33
MODES = 4
SWEEPS = 3
SKY_ROWS = 64
SKY_COLS = 512


def draw_sky_cube(key, part):
    keys = jax.random.split(jax.random.fold_in(key, 11), 3)
    channel_pos = jnp.arange(CHANNELS).astype(jnp.float32)
    log_freq = jnp.log(1.0 + channel_pos / CHANNELS)
    shape_four = (4, SKY_ROWS, SKY_COLS)
    log_amp = jax.random.uniform(keys[0], shape_four, jnp.float32, -1.0, 1.0)
    component_weights = jnp.array([1.0, 0.5, 0.25, 0.125], jnp.float32)
    amplitude = 20.0 * jnp.exp(log_amp) * component_weights[:, None, None]
    spectral = 2.5 + jax.random.uniform(keys[1], shape_four, jnp.float32, -0.5, 0.5)
    noise = 8.0 * jax.random.truncated_normal(keys[2], -4.0, 4.0, (CHANNELS, SKY_ROWS, SKY_COLS), jnp.float32)
    foreground = noise
    for component in range(4):
        foreground = foreground + amplitude[component][None] * jnp.exp(-spectral[component][None] * log_freq[:, None, None])
    return foreground


def draw_beam_taps(key, part):
    keys = jax.random.split(jax.random.fold_in(key, 23), 2)
    spread = 4.0 + 5.0 * jax.random.uniform(keys[0], (CHANNELS, 1), jnp.float32)
    offset = jnp.arange(TAPS).astype(jnp.float32) - TAPS // 2
    jitter = 0.6 + 0.8 * jax.random.uniform(keys[1], (CHANNELS, TAPS), jnp.float32)
    return jnp.exp(-offset[None, :] ** 2 / (2.0 * spread ** 2)) * jitter / (2.5 * spread)


def setup_inputs(seed: int = 0, part: int = 0) -> dict:
    streams_of = jax.random.split(jax.random.key(seed), 3)
    own_keys = jax.random.split(jax.random.fold_in(streams_of[2], part), 3)
    sky_cube = draw_sky_cube(jax.random.fold_in(jax.random.fold_in(streams_of[2], part), 71), part)
    beam_taps = draw_beam_taps(jax.random.fold_in(streams_of[2], 71), part)
    return {"sky_cube": sky_cube, "beam_taps": beam_taps}


def convolve(padded_field, beam_taps, axis_dim, out_width):
    result = None
    for offset in range(beam_taps.shape[1]):
        piece = lax.slice_in_dim(padded_field, offset, offset + out_width, axis=axis_dim)
        term = beam_taps[:, offset][:, None, None] * piece
        result = term if result is None else result + term
    return result

def orthonormalize(block):
    length = block.shape[0]
    columns = []
    for index in range(block.shape[1]):
        vector = block[:, index]
        for repeat in range(2):
            for earlier in columns:
                vector = vector - jnp.sum(earlier * vector) * earlier
        scale_mean = jnp.mean(vector * vector) + 1e-06
        vector = vector / jnp.sqrt(scale_mean) / jnp.sqrt(jnp.float32(length))
        columns.append(vector)
    return jnp.stack(columns, axis=1)

def leading_modes(gram_matrix, channels):
    scaled_gram = gram_matrix * (channels / jnp.trace(gram_matrix))
    channel_pos = jnp.arange(channels).astype(jnp.float32)
    mode_index = jnp.arange(MODES).astype(jnp.float32)
    cosine_basis = jnp.cos(jnp.pi * mode_index[None, :] * (channel_pos[:, None] + 0.5) / channels)
    basis = orthonormalize(cosine_basis)
    for sweep in range(SWEEPS):
        basis = orthonormalize(jnp.dot(scaled_gram, basis, precision=lax.Precision.HIGHEST, preferred_element_type=jnp.float32))
    return basis

def reference(sky_cube, beam_taps):
    margin = TAPS // 2
    channels, sky_rows, sky_cols = sky_cube.shape
    padded_cols = jnp.pad(sky_cube, ((0, 0), (0, 0), (margin, margin)))
    smoothed = convolve(padded_cols, beam_taps, 2, sky_cols)
    padded_rows = jnp.pad(smoothed, ((0, 0), (margin, margin), (0, 0)))
    beamed = convolve(padded_rows, beam_taps, 1, sky_rows)
    flattened = beamed.reshape(channels, sky_rows * sky_cols)
    gram_matrix = jnp.dot(flattened, flattened.T, precision=lax.Precision.HIGHEST, preferred_element_type=jnp.float32)
    mode_spectra = leading_modes(gram_matrix, channels)
    coefficients = jnp.dot(mode_spectra.T, flattened, precision=lax.Precision.HIGHEST, preferred_element_type=jnp.float32)
    cleaned = flattened - jnp.dot(mode_spectra, coefficients, precision=lax.Precision.HIGHEST, preferred_element_type=jnp.float32)
    return cleaned.reshape(channels, sky_rows, sky_cols)
```

```python
import functools

import jax
import jax.numpy as jnp
from jax import lax
from jax.experimental import pallas as pl
from jax.experimental.pallas import tpu as pltpu
from jax.sharding import PartitionSpec as P

MODES = 4
SWEEPS = 3
LANES = 128
SUB = 8

ANY = pl.BlockSpec(memory_space=pl.ANY)
VM = pl.BlockSpec(memory_space=pltpu.VMEM)
SM = pl.BlockSpec(memory_space=pltpu.SMEM)
f32 = jnp.float32


def shape(*dims):
    return jax.ShapeDtypeStruct(dims, f32)


def cost(flops, nbytes):
    return pl.CostEstimate(flops=int(flops), bytes_accessed=int(nbytes), transcendentals=0)


def row_taps(buf, taps_ref, out_ref, rows, cols, taps):
    def body(group, carry):
        part = pl.ds(pl.multiple_of(group * SUB, SUB), SUB)
        weights = [taps_ref[a] for a in range(taps)]
        total = [None] * rows
        for r in range(rows + taps - 1):
            x = buf[r, part, :]
            for i in range(max(0, r - taps + 1), min(rows - 1, r) + 1):
                term = weights[r - i] * x
                total[i] = term if total[i] is None else total[i] + term
        for i in range(rows):
            out_ref[i, part, :] = total[i]
        return carry

    lax.fori_loop(0, cols // SUB, body, 0)


def col_taps(buf, taps_ref, out_ref, rows, cols, taps, step=2):
    groups = cols // SUB

    def body(block, carry):
        weights = [taps_ref[a] for a in range(taps)]
        total = {}
        for s in range(SUB * (groups - 1) + taps):
            for q in range(step):
                i = block * step + q
                x = buf[i, pl.ds(s, SUB), :]
                for g in range(groups):
                    a = s - SUB * g
                    if 0 <= a < taps:
                        term = weights[a] * x
                        total[q, g] = term if a == 0 else total[q, g] + term
                        if a == taps - 1:
                            out_ref[i, pl.ds(SUB * g, SUB), :] = total.pop((q, g))
        return carry

    lax.fori_loop(0, rows // step, body, 0)


def copies_in(pairs, sems):
    started = []
    for index, (source, target) in enumerate(pairs):
        copy = pltpu.make_async_copy(source, target, sems.at[index])
        copy.start()
        started.append(copy)
    for copy in started:
        copy.wait()


def prep_kernel(rows, cols, margin, x_ref, raw_ref, first_ref, last_ref):
    for r in range(rows):
        tile = x_ref[pl.ds(r, LANES, stride=rows), :].T
        raw_ref[0, r] = tile
        first_ref[0, r] = tile[:margin]
        last_ref[0, r] = tile[cols - margin:]


def prep(flat, rows, cols, margin, start, count):
    return pl.pallas_call(
        functools.partial(prep_kernel, rows, cols, margin),
        grid=(count,),
        in_specs=[pl.BlockSpec((LANES * rows, cols), lambda k: (k + start, 0))],
        out_specs=[
            pl.BlockSpec((1, rows, cols, LANES), lambda k: (k, 0, 0, 0)),
            pl.BlockSpec((1, rows, margin, LANES), lambda k: (k, 0, 0, 0)),
            pl.BlockSpec((1, rows, margin, LANES), lambda k: (k, 0, 0, 0)),
        ],
        out_shape=[
            shape(count, rows, cols, LANES),
            shape(count, rows, margin, LANES),
            shape(count, rows, margin, LANES),
        ],
        cost_estimate=cost(4e6 * count, 2.5e6 * count),
        name="prep",
    )(flat)


def columns_kernel(which, rows, cols, margin, taps, flip, x_ref, before_ref, after_ref, taps_ref, out_ref, buf, held, sems):
    copies_in(
        [
            (x_ref.at[which], buf.at[:, pl.ds(margin, cols), :]),
            (before_ref.at[which], buf.at[:, pl.ds(0, margin), :]),
            (after_ref.at[which], buf.at[:, pl.ds(margin + cols, margin), :]),
        ],
        sems,
    )
    if not flip:
        col_taps(buf, taps_ref, out_ref, rows, cols, taps)
    else:
        col_taps(buf, taps_ref, held, rows, cols, taps)
        for r in range(rows):
            out_ref[:, r * cols:(r + 1) * cols] = held[r].T


def columns(which, x, before, after, taps, margin, flip):
    _, rows, cols, _ = x.shape
    count = taps.shape[0]
    out = shape(LANES, rows * cols) if flip else shape(rows, cols, LANES)
    return pl.pallas_call(
        functools.partial(columns_kernel, which, rows, cols, margin, count, flip),
        in_specs=[ANY, ANY, ANY, VM],
        out_specs=VM,
        out_shape=out,
        scratch_shapes=[
            pltpu.VMEM((rows, cols + 2 * margin, LANES), f32),
            pltpu.VMEM((rows, cols, LANES), f32),
            pltpu.SemaphoreType.DMA((3,)),
        ],
        cost_estimate=cost(2e7, 2.5e6),
        name="columns",
    )(x, before, after, taps)


def rows_kernel(rows, cols, margin, taps, raw, side_ref, x_ref, near_ref, far_ref, taps_ref, *rest):
    if raw:
        out_ref, first_ref, last_ref, buf, native, sems = rest
    else:
        out_ref, buf, held, sems = rest
    even = side_ref[0] == 0
    near = jnp.where(even, margin + rows, 0)
    far = jnp.where(even, 0, margin + rows)
    if raw:
        copies_in([(x_ref, native.at[0]), (near_ref, native.at[1]), (far_ref, native.at[2])], sems)
        for slot, start in ((0, margin), (1, near), (2, far)):
            for r in range(rows):
                buf[start + r] = native[slot, pl.ds(r, LANES, stride=rows), :].T
        row_taps(buf, taps_ref, out_ref.at[0], rows, cols, taps)
        first_ref[0] = out_ref[0, :, :margin, :]
        last_ref[0] = out_ref[0, :, cols - margin:, :]
    else:
        copies_in(
            [
                (x_ref, buf.at[pl.ds(margin, rows)]),
                (near_ref, buf.at[pl.ds(near, rows)]),
                (far_ref, buf.at[pl.ds(far, rows)]),
            ],
            sems,
        )
        row_taps(buf, taps_ref, held, rows, cols, taps)
        for r in range(rows):
            out_ref[:, r * cols:(r + 1) * cols] = held[r].T


def rows_of(x, near, far, taps, side, rows, cols, margin, raw):
    count = taps.shape[0]
    if raw:
        outs = [shape(1, rows, cols, LANES), shape(1, rows, margin, LANES), shape(1, rows, margin, LANES)]
        extra = pltpu.VMEM((3, LANES * rows, cols), f32)
    else:
        outs = shape(LANES, rows * cols)
        extra = pltpu.VMEM((rows, cols, LANES), f32)
    return pl.pallas_call(
        functools.partial(rows_kernel, rows, cols, margin, count, raw),
        in_specs=[SM, ANY, ANY, ANY, VM],
        out_specs=[VM] * 3 if raw else VM,
        out_shape=outs,
        scratch_shapes=[
            pltpu.VMEM((rows + 2 * margin, cols, LANES), f32),
            extra,
            pltpu.SemaphoreType.DMA((3,)),
        ],
        cost_estimate=cost(2e7, 4e6),
        name="rows_raw" if raw else "rows",
    )(side, x, near, far, taps)


def gram_kernel(chunks, peers, me_ref, *refs):
    xs, outs = refs[:chunks], refs[chunks:chunks + peers]
    high, low, gram, mixed = refs[chunks + peers:]
    for k, x_ref in enumerate(xs):
        x = x_ref[...]
        h = x.astype(jnp.bfloat16)
        high[k * LANES:(k + 1) * LANES, :] = h
        low[k * LANES:(k + 1) * LANES, :] = (x - h.astype(f32)).astype(jnp.bfloat16)
    last = (((1,), (1,)), ((), ()))
    mixed[...] = lax.dot_general(high[...], low[...], last, preferred_element_type=f32)
    gram[...] = lax.dot_general(high[...], high[...], last, preferred_element_type=f32)
    gram[...] += mixed[...] + mixed[...].T
    size = gram.shape[0] // peers
    for d in range(peers):
        piece = me_ref[0] ^ d
        outs[d][...] = gram[pl.ds(pl.multiple_of(piece * size, size), size), :]


def gram_pieces(xs, me, peers):
    chunks = len(xs)
    channels = chunks * LANES
    pixels = xs[0].shape[1]
    return pl.pallas_call(
        functools.partial(gram_kernel, chunks, peers),
        in_specs=[SM] + [VM] * chunks,
        out_specs=[VM] * peers,
        out_shape=[shape(channels // peers, channels)] * peers,
        scratch_shapes=[
            pltpu.VMEM((channels, pixels), jnp.bfloat16),
            pltpu.VMEM((channels, pixels), jnp.bfloat16),
            pltpu.VMEM((channels, channels), f32),
            pltpu.VMEM((channels, channels), f32),
        ],
        cost_estimate=cost(4e9, 5e6),
        name="gram",
    )(me, *xs)


def split_kernel(count, peers, me_ref, *refs):
    parts, outs = refs[:count], refs[count:count + peers]
    total = refs[count + peers]
    value = parts[0][...]
    for part in parts[1:]:
        value = value + part[...]
    total[...] = value
    size = total.shape[0] // peers
    for d in range(peers):
        piece = me_ref[0] ^ d
        outs[d][...] = total[pl.ds(pl.multiple_of(piece * size, size), size), :]


def sum_and_split(parts, me, peers):
    height, width = parts[0].shape
    return pl.pallas_call(
        functools.partial(split_kernel, len(parts), peers),
        in_specs=[SM] + [VM] * len(parts),
        out_specs=[VM] * peers,
        out_shape=[shape(height // peers, width)] * peers,
        scratch_shapes=[pltpu.VMEM((height, width), f32)],
        name="sum_and_split",
    )(me, *parts)


def join_kernel(peers, me_ref, *refs):
    parts, out_ref = refs[:peers], refs[peers]
    size = parts[0].shape[0]
    for d in range(peers):
        piece = me_ref[0] ^ d
        out_ref[pl.ds(pl.multiple_of(piece * size, size), size), :] = parts[d][...]


def join(parts, me):
    peers = len(parts)
    height, width = parts[0].shape
    return pl.pallas_call(
        functools.partial(join_kernel, peers),
        in_specs=[SM] + [VM] * peers,
        out_specs=VM,
        out_shape=shape(height * peers, width),
        name="join",
    )(me, *parts)


def exchange(pieces, axis):
    peers = len(pieces)
    moved = [pieces[0]]
    for d in range(1, peers):
        moved.append(lax.ppermute(pieces[d], axis, [(i, i ^ d) for i in range(peers)]))
    return moved


def dot(u, v):
    return jnp.sum(u * v, axis=1, keepdims=True)


def orthonormal_rows(block, channels):
    done, cross = [], {}
    for index, vector in enumerate(block):
        for repeat in range(2):
            factors = [dot(q, vector) for q in done]
            for j in range(index):
                for i in range(j):
                    factors[j] = factors[j] - factors[i] * cross[i, j]
            for q, factor in zip(done, factors):
                vector = vector - factor * q
        scale_mean = dot(vector, vector) / channels + 1e-06
        vector = vector / jnp.sqrt(scale_mean) / jnp.sqrt(jnp.float32(channels))
        for i, q in enumerate(done):
            cross[i, index] = dot(q, vector)
        done.append(vector)
    return done


def start_kernel(channels, cosine_ref, out_ref):
    rows = orthonormal_rows([cosine_ref[k:k + 1, :] for k in range(MODES)], channels)
    out_ref[...] = jnp.concatenate(rows + [jnp.zeros((SUB - MODES, channels), f32)], axis=0)


def start_basis(channels):
    channel_pos = jnp.arange(channels).astype(f32)
    mode_index = jnp.arange(MODES).astype(f32)
    cosine = jnp.cos(jnp.pi * mode_index[:, None] * (channel_pos[None, :] + 0.5) / channels)
    return pl.pallas_call(
        functools.partial(start_kernel, channels),
        in_specs=[VM],
        out_specs=VM,
        out_shape=shape(SUB, channels),
        name="start_basis",
    )(cosine)


def spread(basis, wide, channels):
    for c in range(0, channels, LANES):
        tall = basis[:, c:c + LANES].T
        for k in range(MODES):
            wide[k, c:c + LANES, :] = jnp.broadcast_to(tall[:, k:k + 1], (LANES, LANES))


def clean_kernel(chunks, peers, rows, cols, me_ref, start_ref, *refs):
    xs, pieces, out_ref = refs[:chunks], refs[chunks:chunks + peers], refs[chunks + peers]
    x_buf, gram, wide, coef, sems, out_buf, out_sems = refs[chunks + peers + 1:]
    channels = chunks * LANES
    started = []
    for k in range(chunks):
        copy = pltpu.make_async_copy(xs[k], x_buf.at[pl.ds(k * LANES, LANES)], sems.at[k])
        copy.start()
        started.append(copy)
    size = channels // peers
    for d in range(peers):
        piece = me_ref[0] ^ d
        gram[pl.ds(pl.multiple_of(piece * size, size), size), :] = pieces[d][...]
    row_id = lax.broadcasted_iota(jnp.int32, (channels, channels), 0)
    col_id = lax.broadcasted_iota(jnp.int32, (channels, channels), 1)
    diagonal = jnp.sum(jnp.where(row_id == col_id, gram[...], 0.0), axis=0, keepdims=True)
    scale = channels / jnp.sum(diagonal, axis=1, keepdims=True)
    basis = start_ref[...]
    for sweep in range(SWEEPS):
        spread(basis, wide, channels)
        totals = [[None] * (channels // LANES) for k in range(MODES)]
        for k in range(MODES):
            for t in range(channels // LANES):
                total = None
                for c in range(0, channels, SUB):
                    term = wide[k, c:c + SUB, :] * gram[c:c + SUB, t * LANES:(t + 1) * LANES]
                    total = term if total is None else total + term
                totals[k][t] = jnp.sum(total, axis=0, keepdims=True)
        vectors = [jnp.concatenate(totals[k], axis=1) * scale for k in range(MODES)]
        new = orthonormal_rows(vectors, channels)
        basis = jnp.concatenate(new + [jnp.zeros((SUB - MODES, channels), f32)], axis=0)
    spread(basis, wide, channels)
    for copy in started:
        copy.wait()

    def one_row(r, carry):
        part = pl.ds(pl.multiple_of(r * cols, cols), cols)
        totals = [None] * MODES
        for c in range(0, channels, SUB):
            x = x_buf[c:c + SUB, part]
            for k in range(MODES):
                term = wide[k, c:c + SUB, :] * x
                totals[k] = term if totals[k] is None else totals[k] + term
        coefs = [jnp.broadcast_to(jnp.sum(total, axis=0, keepdims=True), (SUB, LANES)) for total in totals]
        for c in range(0, channels, SUB):
            value = x_buf[c:c + SUB, part]
            model = wide[0, c:c + SUB, :] * coefs[0]
            for k in range(1, MODES):
                model = model + wide[k, c:c + SUB, :] * coefs[k]
            out_buf[pl.ds(c * rows + r, SUB, stride=rows), :] = value - model
        return carry

    lax.fori_loop(0, rows, one_row, 0)
    copy = pltpu.make_async_copy(out_buf, out_ref, out_sems.at[0])
    copy.start()
    copy.wait()


def clean(xs, pieces, me, start, rows, cols):
    chunks, peers = len(xs), len(pieces)
    channels = chunks * LANES
    return pl.pallas_call(
        functools.partial(clean_kernel, chunks, peers, rows, cols),
        in_specs=[SM, VM] + [ANY] * chunks + [VM] * peers,
        out_specs=ANY,
        out_shape=shape(channels * rows, cols),
        scratch_shapes=[
            pltpu.VMEM((channels, rows * cols), f32),
            pltpu.VMEM((channels, channels), f32),
            pltpu.VMEM((MODES, channels, LANES), f32),
            pltpu.VMEM((SUB, LANES), f32),
            pltpu.SemaphoreType.DMA((chunks,)),
            pltpu.VMEM((channels * rows, cols), f32),
            pltpu.SemaphoreType.DMA((1,)),
        ],
        cost_estimate=cost(4e7, 9e6),
        name="clean",
    )(me, start, *xs, *pieces)


def per_device(sky_cube, beam_taps):
    taps = beam_taps.shape[1]
    margin = taps // 2
    channels, rows, cols = sky_cube.shape
    chunks = channels // LANES
    n_row, n_col = lax.axis_size("row"), lax.axis_size("col")
    me_row = lax.axis_index("row").astype(jnp.int32)
    me_col = lax.axis_index("col").astype(jnp.int32)
    side = jnp.reshape(me_row % 2, (1,))
    near_pairs = [(i, i ^ 1) for i in range(n_row)]
    far_pairs = [(i, ((i + 1) ^ 1) - 1) for i in range(1, n_row - 1)]
    right = [(i, i + 1) for i in range(n_col - 1)]
    left = [(j, i) for i, j in right]

    flat = sky_cube.reshape(channels * rows, cols)
    head = flat[:LANES * rows]
    far0 = lax.ppermute(head, "row", far_pairs)
    near0 = lax.ppermute(head, "row", near_pairs)
    wide_taps = jnp.broadcast_to(
        beam_taps.T.reshape(taps, chunks, 1, LANES).transpose(1, 0, 2, 3), (chunks, taps, SUB, LANES)
    )
    tap = [wide_taps[k] for k in range(chunks)]
    start = start_basis(channels)

    raw, first, last = prep(flat, rows, cols, margin, 1, chunks - 1)
    before = lax.ppermute(last, "col", right)
    after = lax.ppermute(first, "col", left)
    xs = [None] * chunks
    smooth, near, far = [None] * chunks, [None] * chunks, [None] * chunks
    for k in range(1, chunks):
        smooth[k] = columns(k - 1, raw, before, after, tap[k], margin, False)
        far[k] = lax.ppermute(smooth[k], "row", far_pairs)
        near[k] = lax.ppermute(smooth[k], "row", near_pairs)
    mixed, first0, last0 = rows_of(head, near0, far0, tap[0], side, rows, cols, margin, True)
    before0 = lax.ppermute(last0, "col", right)
    after0 = lax.ppermute(first0, "col", left)
    for k in range(1, chunks):
        xs[k] = rows_of(smooth[k], near[k], far[k], tap[k], side, rows, cols, margin, False)
    xs[0] = columns(0, mixed, before0, after0, tap[0], margin, True)

    row_ref, col_ref = jnp.reshape(me_row, (1,)), jnp.reshape(me_col, (1,))
    pieces = exchange(gram_pieces(xs, row_ref, n_row), "row")
    if pieces[0].shape[0] % (SUB * n_col) == 0:
        small = exchange(sum_and_split(pieces, col_ref, n_col), "col")
        mine = functools.reduce(jnp.add, small)
        block = join(exchange([mine] * n_col, "col"), col_ref)
    else:
        mine = functools.reduce(jnp.add, pieces)
        block = functools.reduce(jnp.add, exchange([mine] * n_col, "col"))
    parts = exchange([block] * n_row, "row")
    out = clean(xs, parts, row_ref, start, rows, cols)
    return out.reshape(channels, rows, cols)


def solution(mesh):
    placed = (P(None, ("patch", "row"), "col"), P())
    return jax.shard_map(
        per_device,
        mesh=mesh,
        in_specs=placed,
        out_specs=P(None, ("patch", "row"), "col"),
        check_vma=False,
    )
```

```python
import functools

import jax
import jax.numpy as jnp
from jax import lax
from jax.experimental import pallas as pl
from jax.experimental.pallas import tpu as pltpu
from jax.sharding import PartitionSpec as P

MODES = 4
SWEEPS = 3
LANES = 128
SUB = 8

ANY = pl.BlockSpec(memory_space=pl.ANY)
VM = pl.BlockSpec(memory_space=pltpu.VMEM)
SM = pl.BlockSpec(memory_space=pltpu.SMEM)
f32 = jnp.float32


def shape(*dims):
    return jax.ShapeDtypeStruct(dims, f32)


def cost(flops, nbytes):
    return pl.CostEstimate(flops=int(flops), bytes_accessed=int(nbytes), transcendentals=0)


def row_taps(buf, taps_ref, out_ref, rows, taps, first, count):
    def body(group, carry):
        part = pl.ds(pl.multiple_of(group * SUB, SUB), SUB)
        weights = [taps_ref[a] for a in range(taps)]
        total = [None] * rows
        for r in range(rows + taps - 1):
            x = buf[r, part, :]
            for i in range(max(0, r - taps + 1), min(rows - 1, r) + 1):
                term = weights[r - i] * x
                total[i] = term if total[i] is None else total[i] + term
        for i in range(rows):
            out_ref[i, part, :] = total[i]
        return carry

    lax.fori_loop(first, first + count, body, 0)


def col_taps(buf, taps_ref, out_ref, cols, taps, first, count, step=2):
    groups = cols // SUB

    def body(block, carry):
        weights = [taps_ref[a] for a in range(taps)]
        total = {}
        for s in range(SUB * (groups - 1) + taps):
            for q in range(step):
                i = block * step + q
                x = buf[i, pl.ds(s, SUB), :]
                for g in range(groups):
                    a = s - SUB * g
                    if 0 <= a < taps:
                        term = weights[a] * x
                        total[q, g] = term if a == 0 else total[q, g] + term
                        if a == taps - 1:
                            out_ref[i, pl.ds(SUB * g, SUB), :] = total.pop((q, g))
        return carry

    lax.fori_loop(first // step, (first + count) // step, body, 0)


PARTS = 4


def start_all(pairs, sems):
    started = []
    for index, (source, target) in enumerate(pairs):
        copy = pltpu.make_async_copy(source, target, sems.at[index])
        copy.start()
        started.append(copy)
    return started


def prep_kernel(rows, cols, margin, x_ref, raw_ref, first_ref, last_ref):
    for r in range(rows):
        tile = x_ref[pl.ds(r, LANES, stride=rows), :].T
        raw_ref[0, r] = tile
        first_ref[0, r] = tile[:margin]
        last_ref[0, r] = tile[cols - margin:]


def prep(flat, rows, cols, margin, start, count):
    return pl.pallas_call(
        functools.partial(prep_kernel, rows, cols, margin),
        grid=(count,),
        in_specs=[pl.BlockSpec((LANES * rows, cols), lambda k: (k + start, 0))],
        out_specs=[
            pl.BlockSpec((1, rows, cols, LANES), lambda k: (k, 0, 0, 0)),
            pl.BlockSpec((1, rows, margin, LANES), lambda k: (k, 0, 0, 0)),
            pl.BlockSpec((1, rows, margin, LANES), lambda k: (k, 0, 0, 0)),
        ],
        out_shape=[
            shape(count, rows, cols, LANES),
            shape(count, rows, margin, LANES),
            shape(count, rows, margin, LANES),
        ],
        cost_estimate=cost(4e6 * count, 2.5e6 * count),
        name="prep",
    )(flat)


def columns_kernel(which, rows, cols, margin, taps, flip, x_ref, before_ref, after_ref, taps_ref, out_ref, buf, held, sems):
    share = rows // PARTS
    pairs = []
    for p in range(PARTS):
        part = pl.ds(p * share, share)
        pairs += [
            (x_ref.at[which, part], buf.at[part, pl.ds(margin, cols), :]),
            (before_ref.at[which, part], buf.at[part, pl.ds(0, margin), :]),
            (after_ref.at[which, part], buf.at[part, pl.ds(margin + cols, margin), :]),
        ]
    started = start_all(pairs, sems)
    for p in range(PARTS):
        for copy in started[3 * p:3 * p + 3]:
            copy.wait()
        col_taps(buf, taps_ref.at[0], held if flip else out_ref, cols, taps, p * share, share)
        if flip:
            for r in range(p * share, p * share + share):
                out_ref[:, r * cols:(r + 1) * cols] = held[r].T


def columns(which, x, before, after, wide_taps, chunk, margin, flip):
    _, rows, cols, _ = x.shape
    taps = wide_taps.shape[1]
    out = (LANES, rows * cols) if flip else (rows, cols, LANES)
    return pl.pallas_call(
        functools.partial(columns_kernel, which, rows, cols, margin, taps, flip),
        grid=(1,),
        in_specs=[ANY, ANY, ANY, pl.BlockSpec((1, taps, SUB, LANES), lambda k: (chunk, 0, 0, 0))],
        out_specs=pl.BlockSpec(out, lambda k: (0,) * len(out)),
        out_shape=shape(*out),
        scratch_shapes=[
            pltpu.VMEM((rows, cols + 2 * margin, LANES), f32),
            pltpu.VMEM((rows, cols, LANES), f32),
            pltpu.SemaphoreType.DMA((3 * PARTS,)),
        ],
        cost_estimate=cost(2e7, 2.5e6),
        name="columns",
    )(x, before, after, wide_taps)


def raw_rows_kernel(count, rows, cols, margin, taps, side_ref, x_ref, near_ref, far_ref, taps_ref, out_ref, first_ref, last_ref, buf, native, sems):
    even = side_ref[0] == 0
    near = jnp.where(even, margin + rows, 0)
    far = jnp.where(even, 0, margin + rows)
    height = LANES * rows
    pairs = []
    for n in range(count):
        part = pl.ds(n * height, height)
        for slot, source in enumerate((x_ref, near_ref, far_ref)):
            pairs.append((source.at[part], native.at[n, slot]))
    started = start_all(pairs, sems)
    for n in range(count):
        for slot, start in enumerate((margin, near, far)):
            started[3 * n + slot].wait()
            for r in range(rows):
                buf[start + r] = native[n, slot, pl.ds(r, LANES, stride=rows), :].T
        row_taps(buf, taps_ref.at[n], out_ref.at[n], rows, taps, 0, cols // SUB)
        first_ref[n] = out_ref[n, :, :margin, :]
        last_ref[n] = out_ref[n, :, cols - margin:, :]


def raw_rows(x, near, far, wide_taps, side, rows, cols, margin):
    count = x.shape[0] // (LANES * rows)
    taps = wide_taps.shape[1]
    return pl.pallas_call(
        functools.partial(raw_rows_kernel, count, rows, cols, margin, taps),
        in_specs=[SM, ANY, ANY, ANY, VM],
        out_specs=[VM] * 3,
        out_shape=[
            shape(count, rows, cols, LANES),
            shape(count, rows, margin, LANES),
            shape(count, rows, margin, LANES),
        ],
        scratch_shapes=[
            pltpu.VMEM((rows + 2 * margin, cols, LANES), f32),
            pltpu.VMEM((count, 3, LANES * rows, cols), f32),
            pltpu.SemaphoreType.DMA((3 * count,)),
        ],
        cost_estimate=cost(3e7 * count, 4e6 * count),
        name="raw_rows",
    )(side, x, near, far, wide_taps)


def rows_kernel(rows, cols, margin, taps, side_ref, x_ref, near_ref, far_ref, taps_ref, out_ref, buf, held, sems):
    even = side_ref[0] == 0
    near = jnp.where(even, margin + rows, 0)
    far = jnp.where(even, 0, margin + rows)
    share = cols // PARTS
    pairs = []
    for p in range(PARTS):
        part = pl.ds(p * share, share)
        for source, start in ((x_ref, margin), (near_ref, near), (far_ref, far)):
            pairs.append((source.at[:, part, :], buf.at[pl.ds(start, rows), part, :]))
    started = start_all(pairs, sems)
    for p in range(PARTS):
        for copy in started[3 * p:3 * p + 3]:
            copy.wait()
        row_taps(buf, taps_ref.at[0], held, rows, taps, p * share // SUB, share // SUB)
    for r in range(rows):
        out_ref[:, r * cols:(r + 1) * cols] = held[r].T


def rows_of(x, near, far, wide_taps, chunk, side, margin):
    rows, cols, _ = x.shape
    taps = wide_taps.shape[1]
    return pl.pallas_call(
        functools.partial(rows_kernel, rows, cols, margin, taps),
        grid=(1,),
        in_specs=[SM, ANY, ANY, ANY, pl.BlockSpec((1, taps, SUB, LANES), lambda k: (chunk, 0, 0, 0))],
        out_specs=pl.BlockSpec((LANES, rows * cols), lambda k: (0, 0)),
        out_shape=shape(LANES, rows * cols),
        scratch_shapes=[
            pltpu.VMEM((rows + 2 * margin, cols, LANES), f32),
            pltpu.VMEM((rows, cols, LANES), f32),
            pltpu.SemaphoreType.DMA((3 * PARTS,)),
        ],
        cost_estimate=cost(2e7, 4e6),
        name="rows",
    )(side, x, near, far, wide_taps)


def upper(chunks):
    return [(i, j) for i in range(chunks) for j in range(i, chunks)]


def gram_kernel(chunks, peers, me_ref, *refs):
    xs, outs = refs[:chunks], refs[chunks:chunks + peers]
    high, low, packed = refs[chunks + peers:]
    for k, x_ref in enumerate(xs):
        x = x_ref[...]
        h = x.astype(jnp.bfloat16)
        high[k * LANES:(k + 1) * LANES, :] = h
        low[k * LANES:(k + 1) * LANES, :] = (x - h.astype(f32)).astype(jnp.bfloat16)
    last = (((1,), (1,)), ((), ()))
    mixed = lax.dot_general(high[...], low[...], last, preferred_element_type=f32)
    gram = lax.dot_general(high[...], high[...], last, preferred_element_type=f32)
    for index, (i, j) in enumerate(upper(chunks)):
        a, b = slice(i * LANES, (i + 1) * LANES), slice(j * LANES, (j + 1) * LANES)
        packed[index * LANES:(index + 1) * LANES, :] = gram[a, b] + mixed[a, b] + mixed[b, a].T
    size = packed.shape[0] // peers
    for d in range(peers):
        piece = me_ref[0] ^ d
        outs[d][...] = packed[pl.ds(pl.multiple_of(piece * size, size), size), :]


def gram_pieces(xs, me, peers):
    chunks = len(xs)
    channels, pixels = chunks * LANES, xs[0].shape[1]
    height = len(upper(chunks)) * LANES
    return pl.pallas_call(
        functools.partial(gram_kernel, chunks, peers),
        in_specs=[SM] + [VM] * chunks,
        out_specs=[VM] * peers,
        out_shape=[shape(height // peers, LANES)] * peers,
        scratch_shapes=[
            pltpu.VMEM((channels, pixels), jnp.bfloat16),
            pltpu.VMEM((channels, pixels), jnp.bfloat16),
            pltpu.VMEM((height, LANES), f32),
        ],
        cost_estimate=cost(4e9, 5e6),
        name="gram",
    )(me, *xs)


def split_kernel(count, peers, me_ref, *refs):
    parts, outs = refs[:count], refs[count:count + peers]
    total = refs[count + peers]
    value = parts[0][...]
    for part in parts[1:]:
        value = value + part[...]
    total[...] = value
    size = total.shape[0] // peers
    for d in range(peers):
        piece = me_ref[0] ^ d
        outs[d][...] = total[pl.ds(pl.multiple_of(piece * size, size), size), :]


def sum_and_split(parts, me, peers):
    height, width = parts[0].shape
    return pl.pallas_call(
        functools.partial(split_kernel, len(parts), peers),
        in_specs=[SM] + [VM] * len(parts),
        out_specs=[VM] * peers,
        out_shape=[shape(height // peers, width)] * peers,
        scratch_shapes=[pltpu.VMEM((height, width), f32)],
        name="sum_and_split",
    )(me, *parts)


def join_kernel(peers, me_ref, *refs):
    parts, out_ref = refs[:peers], refs[peers]
    size = parts[0].shape[0]
    for d in range(peers):
        piece = me_ref[0] ^ d
        out_ref[pl.ds(pl.multiple_of(piece * size, size), size), :] = parts[d][...]


def join(parts, me):
    peers = len(parts)
    height, width = parts[0].shape
    return pl.pallas_call(
        functools.partial(join_kernel, peers),
        in_specs=[SM] + [VM] * peers,
        out_specs=VM,
        out_shape=shape(height * peers, width),
        name="join",
    )(me, *parts)


def exchange(pieces, axis):
    peers = len(pieces)
    moved = [pieces[0]]
    for d in range(1, peers):
        moved.append(lax.ppermute(pieces[d], axis, [(i, i ^ d) for i in range(peers)]))
    return moved


def dot(u, v):
    return jnp.sum(u * v, axis=1, keepdims=True)


def orthonormal_rows(block, channels):
    done, cross = [], {}
    for index, vector in enumerate(block):
        for repeat in range(2):
            factors = [dot(q, vector) for q in done]
            for j in range(index):
                for i in range(j):
                    factors[j] = factors[j] - factors[i] * cross[i, j]
            for q, factor in zip(done, factors):
                vector = vector - factor * q
        scale_mean = dot(vector, vector) / channels + 1e-06
        vector = vector / jnp.sqrt(scale_mean) / jnp.sqrt(jnp.float32(channels))
        for i, q in enumerate(done):
            cross[i, index] = dot(q, vector)
        done.append(vector)
    return done


def start_kernel(channels, cosine_ref, out_ref):
    rows = orthonormal_rows([cosine_ref[k:k + 1, :] for k in range(MODES)], channels)
    out_ref[...] = jnp.concatenate(rows + [jnp.zeros((SUB - MODES, channels), f32)], axis=0)


def start_basis(channels):
    channel_pos = jnp.arange(channels).astype(f32)
    mode_index = jnp.arange(MODES).astype(f32)
    cosine = jnp.cos(jnp.pi * mode_index[:, None] * (channel_pos[None, :] + 0.5) / channels)
    return pl.pallas_call(
        functools.partial(start_kernel, channels),
        in_specs=[VM],
        out_specs=VM,
        out_shape=shape(SUB, channels),
        name="start_basis",
    )(cosine)


def spread(basis, wide, channels):
    for c in range(0, channels, LANES):
        tall = basis[:, c:c + LANES].T
        for k in range(MODES):
            wide[k, c:c + LANES, :] = jnp.broadcast_to(tall[:, k:k + 1], (LANES, LANES))


def load_all(xs, x_buf, sems):
    return start_all([(x, x_buf.at[pl.ds(k * LANES, LANES)]) for k, x in enumerate(xs)], sems)


def project(x_buf, wide, part, channels):
    totals = [None] * MODES
    for c in range(0, channels, SUB):
        x = x_buf[c:c + SUB, part]
        for k in range(MODES):
            term = wide[k, c:c + SUB, :] * x
            totals[k] = term if totals[k] is None else totals[k] + term
    return [jnp.broadcast_to(jnp.sum(total, axis=0, keepdims=True), (SUB, LANES)) for total in totals]


def clean_kernel(chunks, peers, rows, cols, me_ref, start_ref, *refs):
    xs, pieces, out_ref = refs[:chunks], refs[chunks:chunks + peers], refs[chunks + peers]
    x_buf, packed, gram, wide, coef, out_buf, sems, out_sems = refs[chunks + peers + 1:]
    channels = chunks * LANES
    started = load_all(xs, x_buf, sems)
    size = packed.shape[0] // peers
    for d in range(peers):
        piece = me_ref[0] ^ d
        packed[pl.ds(pl.multiple_of(piece * size, size), size), :] = pieces[d][...]
    diagonal = jnp.zeros((1, LANES), f32)
    row_id = lax.broadcasted_iota(jnp.int32, (LANES, LANES), 0)
    col_id = lax.broadcasted_iota(jnp.int32, (LANES, LANES), 1)
    for index, (i, j) in enumerate(upper(chunks)):
        block = packed[index * LANES:(index + 1) * LANES, :]
        gram[i * LANES:(i + 1) * LANES, j * LANES:(j + 1) * LANES] = block
        if i != j:
            gram[j * LANES:(j + 1) * LANES, i * LANES:(i + 1) * LANES] = block.T
        else:
            diagonal = diagonal + jnp.sum(jnp.where(row_id == col_id, block, 0.0), axis=0, keepdims=True)
    scale = channels / jnp.sum(diagonal, axis=1, keepdims=True)
    basis = start_ref[...]
    for sweep in range(SWEEPS):
        spread(basis, wide, channels)
        vectors = []
        for k in range(MODES):
            row = []
            for t in range(chunks):
                lanes = slice(t * LANES, (t + 1) * LANES)
                total = None
                for c in range(0, channels, SUB):
                    term = wide[k, c:c + SUB, :] * gram[c:c + SUB, lanes]
                    total = term if total is None else total + term
                row.append(jnp.sum(total, axis=0, keepdims=True))
            vectors.append(jnp.concatenate(row, axis=1) * scale)
        new = orthonormal_rows(vectors, channels)
        basis = jnp.concatenate(new + [jnp.zeros((SUB - MODES, channels), f32)], axis=0)
    spread(basis, wide, channels)
    for copy in started:
        copy.wait()

    def coefficients(r, carry):
        values = project(x_buf, wide, pl.ds(pl.multiple_of(r * cols, cols), cols), channels)
        for k in range(MODES):
            coef[r, k] = values[k]
        return carry

    lax.fori_loop(0, rows, coefficients, 0)
    copies = []
    for n in range(chunks):
        def subtract(r, carry):
            part = pl.ds(pl.multiple_of(r * cols, cols), cols)
            factors = [coef[r, k] for k in range(MODES)]
            for c in range(n * LANES, (n + 1) * LANES, SUB):
                model = wide[0, c:c + SUB, :] * factors[0]
                for k in range(1, MODES):
                    model = model + wide[k, c:c + SUB, :] * factors[k]
                out_buf[pl.ds(c * rows + r, SUB, stride=rows), :] = x_buf[c:c + SUB, part] - model
            return carry

        lax.fori_loop(0, rows, subtract, 0)
        block = pl.ds(n * LANES * rows, LANES * rows)
        copy = pltpu.make_async_copy(out_buf.at[block], out_ref.at[block], out_sems.at[n])
        copy.start()
        copies.append(copy)
    for copy in copies:
        copy.wait()


def clean(xs, pieces, me, start, rows, cols):
    chunks, channels = len(xs), len(xs) * LANES
    return pl.pallas_call(
        functools.partial(clean_kernel, chunks, len(pieces), rows, cols),
        in_specs=[SM, VM] + [ANY] * chunks + [VM] * len(pieces),
        out_specs=ANY,
        out_shape=shape(channels * rows, cols),
        scratch_shapes=[
            pltpu.VMEM((channels, rows * cols), f32),
            pltpu.VMEM((len(upper(chunks)) * LANES, LANES), f32),
            pltpu.VMEM((channels, channels), f32),
            pltpu.VMEM((MODES, channels, LANES), f32),
            pltpu.VMEM((rows, MODES, SUB, LANES), f32),
            pltpu.VMEM((channels * rows, cols), f32),
            pltpu.SemaphoreType.DMA((chunks,)),
            pltpu.SemaphoreType.DMA((chunks,)),
        ],
        cost_estimate=cost(4e7, 9e6),
        name="clean",
    )(me, start, *xs, *pieces)


def per_device(sky_cube, beam_taps):
    taps = beam_taps.shape[1]
    margin = taps // 2
    channels, rows, cols = sky_cube.shape
    chunks = channels // LANES
    n_row, n_col = lax.axis_size("row"), lax.axis_size("col")
    me_row = lax.axis_index("row").astype(jnp.int32)
    me_col = lax.axis_index("col").astype(jnp.int32)
    side = jnp.reshape(me_row % 2, (1,))
    near_pairs = [(i, i ^ 1) for i in range(n_row)]
    far_pairs = [(i, ((i + 1) ^ 1) - 1) for i in range(1, n_row - 1)]
    right = [(i, i + 1) for i in range(n_col - 1)]
    left = [(j, i) for i, j in right]

    height = LANES * rows
    flat = sky_cube.reshape(channels * rows, cols)
    ahead = chunks // 2
    head = flat[:ahead * height]
    head, body = lax.optimization_barrier((head, flat))
    far_head = lax.ppermute(head, "row", far_pairs)
    near_head = lax.ppermute(head, "row", near_pairs)
    wide_taps = jnp.broadcast_to(
        beam_taps.T.reshape(taps, chunks, 1, LANES).transpose(1, 0, 2, 3), (chunks, taps, SUB, LANES)
    )
    start = start_basis(channels)

    raw, first, last = prep(body, rows, cols, margin, ahead, chunks - ahead)
    before = lax.ppermute(last, "col", right)
    after = lax.ppermute(first, "col", left)
    raw, wide_taps, start = lax.optimization_barrier((raw, wide_taps, start))
    xs = [None] * chunks
    smooth, near, far = [None] * chunks, [None] * chunks, [None] * chunks
    for k in range(ahead, chunks):
        smooth[k] = columns(k - ahead, raw, before, after, wide_taps, k, margin, False)
        far[k] = lax.ppermute(smooth[k], "row", far_pairs)
        near[k] = lax.ppermute(smooth[k], "row", near_pairs)
    mixed, first_head, last_head = raw_rows(head, near_head, far_head, wide_taps, side, rows, cols, margin)
    before_head = lax.ppermute(last_head, "col", right)
    after_head = lax.ppermute(first_head, "col", left)
    for k in range(ahead, chunks - 1):
        xs[k] = rows_of(smooth[k], near[k], far[k], wide_taps, k, side, margin)
    for k in range(ahead):
        xs[k] = columns(k, mixed, before_head, after_head, wide_taps, k, margin, True)
    k = chunks - 1
    xs[k] = rows_of(smooth[k], near[k], far[k], wide_taps, k, side, margin)

    row_ref, col_ref = jnp.reshape(me_row, (1,)), jnp.reshape(me_col, (1,))
    pieces = exchange(gram_pieces(xs, row_ref, n_row), "row")
    if pieces[0].shape[0] % (SUB * n_col) == 0:
        small = exchange(sum_and_split(pieces, col_ref, n_col), "col")
        mine = functools.reduce(jnp.add, small)
        block = join(exchange([mine] * n_col, "col"), col_ref)
    else:
        mine = functools.reduce(jnp.add, pieces)
        block = functools.reduce(jnp.add, exchange([mine] * n_col, "col"))
    out = clean(xs, exchange([block] * n_row, "row"), row_ref, start, rows, cols)
    return out.reshape(channels, rows, cols)


def solution(mesh):
    placed = (P(None, ("patch", "row"), "col"), P())
    return jax.shard_map(
        per_device,
        mesh=mesh,
        in_specs=placed,
        out_specs=P(None, ("patch", "row"), "col"),
        check_vma=False,
    )
```

```python
import functools

import jax
import jax.numpy as jnp
from jax import lax
from jax.experimental import pallas as pl
from jax.experimental.pallas import tpu as pltpu
from jax.sharding import PartitionSpec as P

MODES = 4
SWEEPS = 3
LANES = 128
SUB = 8

ANY = pl.BlockSpec(memory_space=pl.ANY)
VM = pl.BlockSpec(memory_space=pltpu.VMEM)
SM = pl.BlockSpec(memory_space=pltpu.SMEM)
f32 = jnp.float32
GRANT = pltpu.CompilerParams(vmem_limit_bytes=24 * 2**20)


def shape(*dims):
    return jax.ShapeDtypeStruct(dims, f32)


def cost(flops, nbytes):
    return pl.CostEstimate(flops=int(flops), bytes_accessed=int(nbytes), transcendentals=0)


PHASES = ((0, 1, 2, 3), (0, 1), (2, 3), (0, 2), (0,), (2,), (1, 3), (1,), (3,))


def short_count(combo, taps):
    return max(len(range(p, taps, 4)) for p in PHASES[combo])


def padded_taps(beam_taps, chunks):
    channels, taps = beam_taps.shape
    height = -(-4 * short_count(0, taps) // SUB) * SUB
    return jnp.pad(beam_taps, ((0, 0), (0, height - taps))).reshape(chunks, LANES, height).transpose(0, 2, 1)


def short_taps(taps_ref, short, taps):
    depth = short_count(0, taps)
    phases = [taps_ref[pl.ds(p, depth, stride=4), :] for p in range(4)]
    for index, combo in enumerate(PHASES):
        short[index * depth:(index + 1) * depth, :] = functools.reduce(jnp.add, [phases[p] for p in combo])


def short_scratch(taps):
    return pltpu.VMEM((len(PHASES) * short_count(0, taps), LANES), f32)


def tap(taps_ref, index):
    return jnp.broadcast_to(taps_ref[index:index + 1, :], (SUB, LANES))


def halves(even, odd):
    return [odd, [p - q for p, q in zip(even, odd)], [p - q for p, q in zip(even[1:], odd)]]


def add_to(total, term):
    return term if total is None else total + term


def row_taps(buf, taps_ref, out_ref, rows, taps, first, count):
    depth = short_count(0, taps)

    def body(group, carry):
        part = pl.ds(pl.multiple_of(group * SUB, SUB), SUB)
        x = [buf[r, part, :] for r in range(rows + taps - 1)]
        base = None
        for s, z in enumerate(halves(x[0::2], x[1::2])):
            sums = []
            for t, w in enumerate(halves(z[0::2], z[1::2])):
                combo = 3 * s + t
                totals = [None] * (rows // 4)
                for k in range(short_count(combo, taps)):
                    weight = tap(taps_ref, combo * depth + k)
                    totals = [add_to(total, weight * w[n + k]) for n, total in enumerate(totals)]
                sums.append(totals)
            both = []
            for n in range(rows // 4):
                both += [sums[0][n] + sums[1][n], sums[0][n] + sums[2][n]]
            if s == 0:
                base = both
            else:
                for m in range(rows // 2):
                    out_ref[2 * m + s - 1, part, :] = base[m] + both[m]
        return carry

    lax.fori_loop(first, first + count, body, 0)


def col_taps(buf, taps_ref, out_ref, streams, cols, taps, first, count, step=2):
    depth = short_count(0, taps)
    groups = cols // (4 * SUB)
    length = streams.shape[2]

    def body(block, carry):
        for q in range(step):
            i = block * step + q
            for m in range(0, length, SUB):
                p = [buf[i, pl.ds(4 * m + d, SUB, stride=4), :] for d in range(7)]
                z = [
                    (p[1], p[3], p[5]),
                    (p[0] - p[1], p[2] - p[3], p[4] - p[5]),
                    (p[2] - p[1], p[4] - p[3], p[6] - p[5]),
                ]
                for s, (even, odd, after) in enumerate(z):
                    streams[q, 3 * s, pl.ds(m, SUB), :] = odd
                    streams[q, 3 * s + 1, pl.ds(m, SUB), :] = even - odd
                    streams[q, 3 * s + 2, pl.ds(m, SUB), :] = after - odd
        where = [(q, g) for q in range(step) for g in range(groups)]
        base = None
        for s in range(3):
            sums = []
            for t in range(3):
                combo = 3 * s + t
                totals = [None] * len(where)
                for k in range(short_count(combo, taps)):
                    weight = tap(taps_ref, combo * depth + k)
                    totals = [
                        add_to(total, weight * streams[q, combo, pl.ds(SUB * g + k, SUB), :])
                        for total, (q, g) in zip(totals, where)
                    ]
                sums.append(totals)
            both = [[sums[0][n] + sums[1 + odd][n] for odd in range(2)] for n in range(len(where))]
            if s == 0:
                base = both
            else:
                for n, (q, g) in enumerate(where):
                    for odd in range(2):
                        at = pl.ds(4 * SUB * g + 2 * odd + s - 1, SUB, stride=4)
                        out_ref[block * step + q, at, :] = base[n][odd] + both[n][odd]
        return carry

    lax.fori_loop(first // step, (first + count) // step, body, 0)


PARTS = 4


def start_all(pairs, sems):
    started = []
    for index, (source, target) in enumerate(pairs):
        copy = pltpu.make_async_copy(source, target, sems.at[index])
        copy.start()
        started.append(copy)
    return started


def prep_kernel(rows, cols, margin, x_ref, raw_ref, first_ref, last_ref):
    for r in range(rows):
        tile = x_ref[pl.ds(r, LANES, stride=rows), :].T
        raw_ref[0, r] = tile
        first_ref[0, r] = tile[:margin]
        last_ref[0, r] = tile[cols - margin:]


def prep(flat, rows, cols, margin, start, count):
    return pl.pallas_call(
        functools.partial(prep_kernel, rows, cols, margin),
        grid=(count,),
        in_specs=[pl.BlockSpec((LANES * rows, cols), lambda k: (k + start, 0))],
        out_specs=[
            pl.BlockSpec((1, rows, cols, LANES), lambda k: (k, 0, 0, 0)),
            pl.BlockSpec((1, rows, margin, LANES), lambda k: (k, 0, 0, 0)),
            pl.BlockSpec((1, rows, margin, LANES), lambda k: (k, 0, 0, 0)),
        ],
        out_shape=[
            shape(count, rows, cols, LANES),
            shape(count, rows, margin, LANES),
            shape(count, rows, margin, LANES),
        ],
        cost_estimate=cost(4e6 * count, 2.5e6 * count),
        compiler_params=GRANT,
        name="prep",
    )(flat)


def columns_kernel(which, rows, cols, margin, taps, flip, x_ref, before_ref, after_ref, taps_ref, out_ref, buf, held, streams, short, sems):
    share = rows // PARTS
    pairs = []
    for p in range(PARTS):
        part = pl.ds(p * share, share)
        pairs += [
            (x_ref.at[which, part], buf.at[part, pl.ds(margin, cols), :]),
            (before_ref.at[which, part], buf.at[part, pl.ds(0, margin), :]),
            (after_ref.at[which, part], buf.at[part, pl.ds(margin + cols, margin), :]),
        ]
    started = start_all(pairs, sems)
    short_taps(taps_ref.at[0], short, taps)
    for p in range(PARTS):
        for copy in started[3 * p:3 * p + 3]:
            copy.wait()
        col_taps(buf, short, held if flip else out_ref, streams, cols, taps, p * share, share)
        if flip:
            for r in range(p * share, p * share + share):
                out_ref[:, r * cols:(r + 1) * cols] = held[r].T


def columns(which, x, before, after, wide_taps, chunk, margin, flip):
    _, rows, cols, _ = x.shape
    taps = 2 * margin + 1
    out = (LANES, rows * cols) if flip else (rows, cols, LANES)
    return pl.pallas_call(
        functools.partial(columns_kernel, which, rows, cols, margin, taps, flip),
        grid=(1,),
        in_specs=[ANY, ANY, ANY, pl.BlockSpec((1,) + wide_taps.shape[1:], lambda k: (chunk, 0, 0))],
        out_specs=pl.BlockSpec(out, lambda k: (0,) * len(out)),
        out_shape=shape(*out),
        scratch_shapes=[
            pltpu.VMEM((rows, cols + 2 * margin + SUB, LANES), f32),
            pltpu.VMEM((rows, cols, LANES), f32),
            pltpu.VMEM((2, len(PHASES), (cols + 2 * margin) // 4, LANES), f32),
            short_scratch(taps),
            pltpu.SemaphoreType.DMA((3 * PARTS,)),
        ],
        cost_estimate=cost(2e7, 2.5e6),
        compiler_params=GRANT,
        name="columns",
    )(x, before, after, wide_taps)


def raw_rows_kernel(count, rows, cols, margin, taps, side_ref, x_ref, near_ref, far_ref, taps_ref, out_ref, first_ref, last_ref, buf, native, short, sems):
    even = side_ref[0] == 0
    near = jnp.where(even, margin + rows, 0)
    far = jnp.where(even, 0, margin + rows)
    height = LANES * rows
    pairs = []
    for n in range(count):
        part = pl.ds(n * height, height)
        for slot, source in enumerate((x_ref, near_ref, far_ref)):
            pairs.append((source.at[part], native.at[n, slot]))
    started = start_all(pairs, sems)
    for n in range(count):
        for slot, start in enumerate((margin, near, far)):
            started[3 * n + slot].wait()
            for r in range(rows):
                buf[start + r] = native[n, slot, pl.ds(r, LANES, stride=rows), :].T
        short_taps(taps_ref.at[n], short, taps)
        row_taps(buf, short, out_ref.at[n], rows, taps, 0, cols // SUB)
        first_ref[n] = out_ref[n, :, :margin, :]
        last_ref[n] = out_ref[n, :, cols - margin:, :]


def raw_rows(x, near, far, wide_taps, side, rows, cols, margin):
    count = x.shape[0] // (LANES * rows)
    taps = 2 * margin + 1
    return pl.pallas_call(
        functools.partial(raw_rows_kernel, count, rows, cols, margin, taps),
        in_specs=[SM, ANY, ANY, ANY, VM],
        out_specs=[VM] * 3,
        out_shape=[
            shape(count, rows, cols, LANES),
            shape(count, rows, margin, LANES),
            shape(count, rows, margin, LANES),
        ],
        scratch_shapes=[
            pltpu.VMEM((rows + 2 * margin, cols, LANES), f32),
            pltpu.VMEM((count, 3, LANES * rows, cols), f32),
            short_scratch(taps),
            pltpu.SemaphoreType.DMA((3 * count,)),
        ],
        cost_estimate=cost(3e7 * count, 4e6 * count),
        compiler_params=GRANT,
        name="raw_rows",
    )(side, x, near, far, wide_taps)


def rows_kernel(rows, cols, margin, taps, side_ref, x_ref, near_ref, far_ref, taps_ref, out_ref, buf, held, short, sems):
    even = side_ref[0] == 0
    near = jnp.where(even, margin + rows, 0)
    far = jnp.where(even, 0, margin + rows)
    share = cols // PARTS
    pairs = []
    for p in range(PARTS):
        part = pl.ds(p * share, share)
        for source, start in ((x_ref, margin), (near_ref, near), (far_ref, far)):
            pairs.append((source.at[:, part, :], buf.at[pl.ds(start, rows), part, :]))
    started = start_all(pairs, sems)
    short_taps(taps_ref.at[0], short, taps)
    for p in range(PARTS):
        for copy in started[3 * p:3 * p + 3]:
            copy.wait()
        row_taps(buf, short, held, rows, taps, p * share // SUB, share // SUB)
    for r in range(rows):
        out_ref[:, r * cols:(r + 1) * cols] = held[r].T


def rows_of(x, near, far, wide_taps, chunk, side, margin):
    rows, cols, _ = x.shape
    taps = 2 * margin + 1
    return pl.pallas_call(
        functools.partial(rows_kernel, rows, cols, margin, taps),
        grid=(1,),
        in_specs=[SM, ANY, ANY, ANY, pl.BlockSpec((1,) + wide_taps.shape[1:], lambda k: (chunk, 0, 0))],
        out_specs=pl.BlockSpec((LANES, rows * cols), lambda k: (0, 0)),
        out_shape=shape(LANES, rows * cols),
        scratch_shapes=[
            pltpu.VMEM((rows + 2 * margin, cols, LANES), f32),
            pltpu.VMEM((rows, cols, LANES), f32),
            short_scratch(taps),
            pltpu.SemaphoreType.DMA((3 * PARTS,)),
        ],
        cost_estimate=cost(2e7, 4e6),
        compiler_params=GRANT,
        name="rows",
    )(side, x, near, far, wide_taps)


def upper(chunks):
    return [(i, j) for i in range(chunks) for j in range(i, chunks)]


def gram_kernel(chunks, peers, me_ref, cosine_ref, *refs):
    xs, outs = refs[:chunks], refs[chunks:chunks + peers]
    start_ref, high, low, packed = refs[chunks + peers:]
    channels = chunks * LANES
    start = orthonormal_rows([cosine_ref[k:k + 1, :] for k in range(MODES)], channels)
    start_ref[...] = jnp.concatenate(start + [jnp.zeros((SUB - MODES, channels), f32)], axis=0)
    for k, x_ref in enumerate(xs):
        x = x_ref[...]
        h = x.astype(jnp.bfloat16)
        high[k * LANES:(k + 1) * LANES, :] = h
        low[k * LANES:(k + 1) * LANES, :] = (x - h.astype(f32)).astype(jnp.bfloat16)
    last = (((1,), (1,)), ((), ()))
    mixed = lax.dot_general(high[...], low[...], last, preferred_element_type=f32)
    gram = lax.dot_general(high[...], high[...], last, preferred_element_type=f32)
    for index, (i, j) in enumerate(upper(chunks)):
        a, b = slice(i * LANES, (i + 1) * LANES), slice(j * LANES, (j + 1) * LANES)
        packed[index * LANES:(index + 1) * LANES, :] = gram[a, b] + mixed[a, b] + mixed[b, a].T
    size = packed.shape[0] // peers
    for d in range(peers):
        piece = me_ref[0] ^ d
        outs[d][...] = packed[pl.ds(pl.multiple_of(piece * size, size), size), :]


def gram_pieces(xs, cosine, me, peers):
    chunks = len(xs)
    channels, pixels = chunks * LANES, xs[0].shape[1]
    height = len(upper(chunks)) * LANES
    return pl.pallas_call(
        functools.partial(gram_kernel, chunks, peers),
        in_specs=[SM, VM] + [VM] * chunks,
        out_specs=[VM] * (peers + 1),
        out_shape=[shape(height // peers, LANES)] * peers + [shape(SUB, channels)],
        scratch_shapes=[
            pltpu.VMEM((channels, pixels), jnp.bfloat16),
            pltpu.VMEM((channels, pixels), jnp.bfloat16),
            pltpu.VMEM((height, LANES), f32),
        ],
        cost_estimate=cost(4e9, 5e6),
        compiler_params=GRANT,
        name="gram",
    )(me, cosine, *xs)


def split_kernel(count, peers, me_ref, *refs):
    parts, outs = refs[:count], refs[count:count + peers]
    held, total, sems = refs[count + peers:]
    for copy in start_all([(part, held.at[n]) for n, part in enumerate(parts)], sems):
        copy.wait()
    value = held[0]
    for n in range(1, count):
        value = value + held[n]
    total[...] = value
    size = total.shape[0] // peers
    for d in range(peers):
        piece = me_ref[0] ^ d
        outs[d][...] = total[pl.ds(pl.multiple_of(piece * size, size), size), :]


def sum_and_split(parts, me, peers):
    height, width = parts[0].shape
    return pl.pallas_call(
        functools.partial(split_kernel, len(parts), peers),
        in_specs=[SM] + [ANY] * len(parts),
        out_specs=[VM] * peers,
        out_shape=[shape(height // peers, width)] * peers,
        scratch_shapes=[
            pltpu.VMEM((len(parts), height, width), f32),
            pltpu.VMEM((height, width), f32),
            pltpu.SemaphoreType.DMA((len(parts),)),
        ],
        compiler_params=GRANT,
        name="sum_and_split",
    )(me, *parts)


def place(pieces, target, me, sems):
    size = target.shape[0] // len(pieces)
    pairs = []
    for d, piece in enumerate(pieces):
        pairs.append((piece, target.at[pl.ds(pl.multiple_of((me ^ d) * size, size), size)]))
    return start_all(pairs, sems)


def join_kernel(peers, me_ref, *refs):
    for copy in place(refs[:peers], refs[peers], me_ref[0], refs[peers + 1]):
        copy.wait()


def join(parts, me):
    peers = len(parts)
    height, width = parts[0].shape
    return pl.pallas_call(
        functools.partial(join_kernel, peers),
        in_specs=[SM] + [ANY] * peers,
        out_specs=VM,
        out_shape=shape(height * peers, width),
        scratch_shapes=[pltpu.SemaphoreType.DMA((peers,))],
        compiler_params=GRANT,
        name="join",
    )(me, *parts)


def exchange(pieces, axis):
    peers = len(pieces)
    moved = [pieces[0]]
    for d in range(1, peers):
        moved.append(lax.ppermute(pieces[d], axis, [(i, i ^ d) for i in range(peers)]))
    return moved


def dot(u, v):
    return jnp.sum(u * v, axis=1, keepdims=True)


def orthonormal_rows(block, channels):
    done, cross = [], {}
    for index, vector in enumerate(block):
        for repeat in range(2):
            factors = [dot(q, vector) for q in done]
            for j in range(index):
                for i in range(j):
                    factors[j] = factors[j] - factors[i] * cross[i, j]
            for q, factor in zip(done, factors):
                vector = vector - factor * q
        scale_mean = dot(vector, vector) / channels + 1e-06
        vector = vector / jnp.sqrt(scale_mean) / jnp.sqrt(jnp.float32(channels))
        for i, q in enumerate(done):
            cross[i, index] = dot(q, vector)
        done.append(vector)
    return done


def cosine_rows(channels):
    channel_pos = jnp.arange(channels).astype(f32)
    mode_index = jnp.arange(MODES).astype(f32)
    return jnp.cos(jnp.pi * mode_index[:, None] * (channel_pos[None, :] + 0.5) / channels)


def spread(basis, wide, channels):
    for c in range(0, channels, LANES):
        tall = basis[:, c:c + LANES].T
        for k in range(MODES):
            wide[k, c:c + LANES, :] = jnp.broadcast_to(tall[:, k:k + 1], (LANES, LANES))


def load_all(xs, x_buf, sems):
    return start_all([(x, x_buf.at[pl.ds(k * LANES, LANES)]) for k, x in enumerate(xs)], sems)


def project(x_buf, wide, part, channels):
    totals = [None] * MODES
    for c in range(0, channels, SUB):
        x = x_buf[c:c + SUB, part]
        for k in range(MODES):
            term = wide[k, c:c + SUB, :] * x
            totals[k] = term if totals[k] is None else totals[k] + term
    return [jnp.broadcast_to(jnp.sum(total, axis=0, keepdims=True), (SUB, LANES)) for total in totals]


def clean_kernel(chunks, peers, rows, cols, me_ref, start_ref, *refs):
    xs, pieces, out_ref = refs[:chunks], refs[chunks:chunks + peers], refs[chunks + peers]
    x_buf, packed, gram, wide, coef, out_buf, sems, piece_sems, out_sems = refs[chunks + peers + 1:]
    channels = chunks * LANES
    placed = place(pieces, packed, me_ref[0], piece_sems)
    started = load_all(xs, x_buf, sems)
    for copy in placed:
        copy.wait()
    diagonal = jnp.zeros((1, LANES), f32)
    row_id = lax.broadcasted_iota(jnp.int32, (LANES, LANES), 0)
    col_id = lax.broadcasted_iota(jnp.int32, (LANES, LANES), 1)
    for index, (i, j) in enumerate(upper(chunks)):
        block = packed[index * LANES:(index + 1) * LANES, :]
        gram[i * LANES:(i + 1) * LANES, j * LANES:(j + 1) * LANES] = block
        if i != j:
            gram[j * LANES:(j + 1) * LANES, i * LANES:(i + 1) * LANES] = block.T
        else:
            diagonal = diagonal + jnp.sum(jnp.where(row_id == col_id, block, 0.0), axis=0, keepdims=True)
    scale = channels / jnp.sum(diagonal, axis=1, keepdims=True)
    basis = start_ref[...]
    for sweep in range(SWEEPS):
        spread(basis, wide, channels)
        vectors = []
        for k in range(MODES):
            row = []
            for t in range(chunks):
                lanes = slice(t * LANES, (t + 1) * LANES)
                total = None
                for c in range(0, channels, SUB):
                    term = wide[k, c:c + SUB, :] * gram[c:c + SUB, lanes]
                    total = term if total is None else total + term
                row.append(jnp.sum(total, axis=0, keepdims=True))
            vectors.append(jnp.concatenate(row, axis=1) * scale)
        new = orthonormal_rows(vectors, channels)
        basis = jnp.concatenate(new + [jnp.zeros((SUB - MODES, channels), f32)], axis=0)
    spread(basis, wide, channels)
    for copy in started:
        copy.wait()

    def coefficients(r, carry):
        values = project(x_buf, wide, pl.ds(pl.multiple_of(r * cols, cols), cols), channels)
        for k in range(MODES):
            coef[r, k] = values[k]
        return carry

    lax.fori_loop(0, rows, coefficients, 0)
    copies = []
    for n in range(chunks):
        def subtract(r, carry):
            part = pl.ds(pl.multiple_of(r * cols, cols), cols)
            factors = [coef[r, k] for k in range(MODES)]
            for c in range(n * LANES, (n + 1) * LANES, SUB):
                model = wide[0, c:c + SUB, :] * factors[0]
                for k in range(1, MODES):
                    model = model + wide[k, c:c + SUB, :] * factors[k]
                out_buf[pl.ds(c * rows + r, SUB, stride=rows), :] = x_buf[c:c + SUB, part] - model
            return carry

        lax.fori_loop(0, rows, subtract, 0)
        block = pl.ds(n * LANES * rows, LANES * rows)
        copy = pltpu.make_async_copy(out_buf.at[block], out_ref.at[block], out_sems.at[n])
        copy.start()
        copies.append(copy)
    for copy in copies:
        copy.wait()


def clean(xs, pieces, me, start, rows, cols):
    chunks, channels = len(xs), len(xs) * LANES
    return pl.pallas_call(
        functools.partial(clean_kernel, chunks, len(pieces), rows, cols),
        in_specs=[SM, VM] + [ANY] * (chunks + len(pieces)),
        out_specs=ANY,
        out_shape=shape(channels * rows, cols),
        scratch_shapes=[
            pltpu.VMEM((channels, rows * cols), f32),
            pltpu.VMEM((len(upper(chunks)) * LANES, LANES), f32),
            pltpu.VMEM((channels, channels), f32),
            pltpu.VMEM((MODES, channels, LANES), f32),
            pltpu.VMEM((rows, MODES, SUB, LANES), f32),
            pltpu.VMEM((channels * rows, cols), f32),
            pltpu.SemaphoreType.DMA((chunks,)),
            pltpu.SemaphoreType.DMA((len(pieces),)),
            pltpu.SemaphoreType.DMA((chunks,)),
        ],
        cost_estimate=cost(4e7, 9e6),
        compiler_params=GRANT,
        name="clean",
    )(me, start, *xs, *pieces)


def per_device(sky_cube, beam_taps):
    taps = beam_taps.shape[1]
    margin = taps // 2
    channels, rows, cols = sky_cube.shape
    chunks = channels // LANES
    n_row, n_col = lax.axis_size("row"), lax.axis_size("col")
    me_row = lax.axis_index("row").astype(jnp.int32)
    me_col = lax.axis_index("col").astype(jnp.int32)
    side = jnp.reshape(me_row % 2, (1,))
    near_pairs = [(i, i ^ 1) for i in range(n_row)]
    far_pairs = [(i, ((i + 1) ^ 1) - 1) for i in range(1, n_row - 1)]
    right = [(i, i + 1) for i in range(n_col - 1)]
    left = [(j, i) for i, j in right]

    height = LANES * rows
    flat = sky_cube.reshape(channels * rows, cols)
    ahead = chunks // 2
    wide_taps = padded_taps(beam_taps, chunks)
    cosine = cosine_rows(channels)

    head, body = lax.optimization_barrier((flat[:ahead * height], flat))
    far_head = lax.ppermute(head, "row", far_pairs)
    near_head = lax.ppermute(head, "row", near_pairs)
    raw, first, last = prep(body, rows, cols, margin, ahead, chunks - ahead)
    before = lax.ppermute(last, "col", right)
    after = lax.ppermute(first, "col", left)
    raw, wide_taps, cosine = lax.optimization_barrier((raw, wide_taps, cosine))
    xs = [None] * chunks
    smooth, near, far = [None] * chunks, [None] * chunks, [None] * chunks
    for k in range(ahead, chunks):
        smooth[k] = columns(k - ahead, raw, before, after, wide_taps, k, margin, False)
        far[k] = lax.ppermute(smooth[k], "row", far_pairs)
        near[k] = lax.ppermute(smooth[k], "row", near_pairs)
    mixed, first_head, last_head = raw_rows(head, near_head, far_head, wide_taps, side, rows, cols, margin)
    before_head = lax.ppermute(last_head, "col", right)
    after_head = lax.ppermute(first_head, "col", left)
    for k in range(ahead, chunks):
        xs[k] = rows_of(smooth[k], near[k], far[k], wide_taps, k, side, margin)
    for k in range(ahead):
        xs[k] = columns(k, mixed, before_head, after_head, wide_taps, k, margin, True)

    row_ref, col_ref = jnp.reshape(me_row, (1,)), jnp.reshape(me_col, (1,))
    *pieces, start = gram_pieces(xs, cosine, row_ref, n_row)
    pieces = exchange(pieces, "row")
    if pieces[0].shape[0] % (SUB * n_col) == 0:
        small = exchange(sum_and_split(pieces, col_ref, n_col), "col")
        mine = functools.reduce(jnp.add, small)
        block = join(exchange([mine] * n_col, "col"), col_ref)
    else:
        mine = functools.reduce(jnp.add, pieces)
        block = functools.reduce(jnp.add, exchange([mine] * n_col, "col"))
    out = clean(xs, exchange([block] * n_row, "row"), row_ref, start, rows, cols)
    return out.reshape(channels, rows, cols)


def solution(mesh):
    placed = (P(None, ("patch", "row"), "col"), P())
    return jax.shard_map(
        per_device,
        mesh=mesh,
        in_specs=placed,
        out_specs=P(None, ("patch", "row"), "col"),
        check_vma=False,
    )
```

```python
import functools

import jax
import jax.numpy as jnp
from jax import lax
from jax.experimental import pallas as pl
from jax.experimental.pallas import tpu as pltpu
from jax.sharding import PartitionSpec as P

MODES = 4
SWEEPS = 3
LANES = 128
SUB = 8

ANY = pl.BlockSpec(memory_space=pl.ANY)
VM = pl.BlockSpec(memory_space=pltpu.VMEM)
SM = pl.BlockSpec(memory_space=pltpu.SMEM)
f32 = jnp.float32
GRANT = pltpu.CompilerParams(vmem_limit_bytes=16 * 2**20)


def shape(*dims):
    return jax.ShapeDtypeStruct(dims, f32)


def cost(flops, nbytes):
    return pl.CostEstimate(flops=int(flops), bytes_accessed=int(nbytes), transcendentals=0)


PHASES = ((0, 1, 2, 3), (0, 1), (2, 3), (0, 2), (0,), (2,), (1, 3), (1,), (3,))


def short_count(combo, taps):
    return max(len(range(p, taps, 4)) for p in PHASES[combo])


def padded_taps(beam_taps, chunks):
    channels, taps = beam_taps.shape
    height = -(-4 * short_count(0, taps) // SUB) * SUB
    return jnp.pad(beam_taps, ((0, 0), (0, height - taps))).reshape(chunks, LANES, height).transpose(0, 2, 1)


def short_taps(taps_ref, short, taps):
    depth = short_count(0, taps)
    phases = [taps_ref[pl.ds(p, depth, stride=4), :] for p in range(4)]
    for index, combo in enumerate(PHASES):
        short[index * depth:(index + 1) * depth, :] = functools.reduce(jnp.add, [phases[p] for p in combo])


def short_scratch(taps):
    return pltpu.VMEM((len(PHASES) * short_count(0, taps), LANES), f32)


def tap(taps_ref, index):
    return jnp.broadcast_to(taps_ref[index:index + 1, :], (SUB, LANES))


def halves(even, odd):
    return [odd, [p - q for p, q in zip(even, odd)], [p - q for p, q in zip(even[1:], odd)]]


def add_to(total, term):
    return term if total is None else total + term


def row_taps(buf, taps_ref, out_ref, rows, taps, first, count):
    depth = short_count(0, taps)

    def body(group, carry):
        part = pl.ds(pl.multiple_of(group * SUB, SUB), SUB)
        x = [buf[r, part, :] for r in range(rows + taps - 1)]
        base = None
        for s, z in enumerate(halves(x[0::2], x[1::2])):
            sums = []
            for t, w in enumerate(halves(z[0::2], z[1::2])):
                combo = 3 * s + t
                totals = [None] * (rows // 4)
                for k in range(short_count(combo, taps)):
                    weight = tap(taps_ref, combo * depth + k)
                    totals = [add_to(total, weight * w[n + k]) for n, total in enumerate(totals)]
                sums.append(totals)
            both = []
            for n in range(rows // 4):
                both += [sums[0][n] + sums[1][n], sums[0][n] + sums[2][n]]
            if s == 0:
                base = both
            else:
                for m in range(rows // 2):
                    out_ref[2 * m + s - 1, part, :] = base[m] + both[m]
        return carry

    lax.fori_loop(first, first + count, body, 0)


def col_taps(buf, taps_ref, out_ref, streams, cols, taps, first, count, step=2):
    depth = short_count(0, taps)
    groups = cols // (4 * SUB)
    length = streams.shape[2]

    def body(block, carry):
        for q in range(step):
            i = block * step + q
            for m in range(0, length, SUB):
                p = [buf[i, pl.ds(4 * m + d, SUB, stride=4), :] for d in range(7)]
                z = [
                    (p[1], p[3], p[5]),
                    (p[0] - p[1], p[2] - p[3], p[4] - p[5]),
                    (p[2] - p[1], p[4] - p[3], p[6] - p[5]),
                ]
                for s, (even, odd, after) in enumerate(z):
                    streams[q, 3 * s, pl.ds(m, SUB), :] = odd
                    streams[q, 3 * s + 1, pl.ds(m, SUB), :] = even - odd
                    streams[q, 3 * s + 2, pl.ds(m, SUB), :] = after - odd
        where = [(q, g) for q in range(step) for g in range(groups)]
        base = None
        for s in range(3):
            sums = []
            for t in range(3):
                combo = 3 * s + t
                totals = [None] * len(where)
                for k in range(short_count(combo, taps)):
                    weight = tap(taps_ref, combo * depth + k)
                    totals = [
                        add_to(total, weight * streams[q, combo, pl.ds(SUB * g + k, SUB), :])
                        for total, (q, g) in zip(totals, where)
                    ]
                sums.append(totals)
            both = [[sums[0][n] + sums[1 + odd][n] for odd in range(2)] for n in range(len(where))]
            if s == 0:
                base = both
            else:
                for n, (q, g) in enumerate(where):
                    for odd in range(2):
                        at = pl.ds(4 * SUB * g + 2 * odd + s - 1, SUB, stride=4)
                        out_ref[block * step + q, at, :] = base[n][odd] + both[n][odd]
        return carry

    lax.fori_loop(first // step, (first + count) // step, body, 0)


PARTS = 4


def start_all(pairs, sems):
    started = []
    for index, (source, target) in enumerate(pairs):
        copy = pltpu.make_async_copy(source, target, sems.at[index])
        copy.start()
        started.append(copy)
    return started


def prep_kernel(rows, cols, margin, x_ref, raw_ref, first_ref, last_ref):
    for r in range(rows):
        tile = x_ref[pl.ds(r, LANES, stride=rows), :].T
        raw_ref[0, r] = tile
        first_ref[0, r] = tile[:margin]
        last_ref[0, r] = tile[cols - margin:]


def prep(flat, rows, cols, margin, start, count):
    return pl.pallas_call(
        functools.partial(prep_kernel, rows, cols, margin),
        grid=(count,),
        in_specs=[pl.BlockSpec((LANES * rows, cols), lambda k: (k + start, 0))],
        out_specs=[
            pl.BlockSpec((1, rows, cols, LANES), lambda k: (k, 0, 0, 0)),
            pl.BlockSpec((1, rows, margin, LANES), lambda k: (k, 0, 0, 0)),
            pl.BlockSpec((1, rows, margin, LANES), lambda k: (k, 0, 0, 0)),
        ],
        out_shape=[
            shape(count, rows, cols, LANES),
            shape(count, rows, margin, LANES),
            shape(count, rows, margin, LANES),
        ],
        cost_estimate=cost(4e6 * count, 2.5e6 * count),
        compiler_params=GRANT,
        name="prep",
    )(flat)


def columns_kernel(which, rows, cols, margin, taps, flip, x_ref, before_ref, after_ref, taps_ref, out_ref, buf, held, streams, short, sems):
    share = rows // PARTS
    pairs = []
    for p in range(PARTS):
        part = pl.ds(p * share, share)
        pairs += [
            (x_ref.at[which, part], buf.at[part, pl.ds(margin, cols), :]),
            (before_ref.at[which, part], buf.at[part, pl.ds(0, margin), :]),
            (after_ref.at[which, part], buf.at[part, pl.ds(margin + cols, margin), :]),
        ]
    started = start_all(pairs, sems)
    short_taps(taps_ref.at[0], short, taps)
    for p in range(PARTS):
        for copy in started[3 * p:3 * p + 3]:
            copy.wait()
        col_taps(buf, short, held if flip else out_ref, streams, cols, taps, p * share, share)
        if flip:
            for r in range(p * share, p * share + share):
                out_ref[:, r * cols:(r + 1) * cols] = held[r].T


def columns(which, x, before, after, wide_taps, chunk, margin, flip):
    _, rows, cols, _ = x.shape
    taps = 2 * margin + 1
    out = (LANES, rows * cols) if flip else (rows, cols, LANES)
    return pl.pallas_call(
        functools.partial(columns_kernel, which, rows, cols, margin, taps, flip),
        grid=(1,),
        in_specs=[ANY, ANY, ANY, pl.BlockSpec((1,) + wide_taps.shape[1:], lambda k: (chunk, 0, 0))],
        out_specs=pl.BlockSpec(out, lambda k: (0,) * len(out)),
        out_shape=shape(*out),
        scratch_shapes=[
            pltpu.VMEM((rows, cols + 2 * margin + SUB, LANES), f32),
            pltpu.VMEM((rows, cols, LANES), f32),
            pltpu.VMEM((2, len(PHASES), (cols + 2 * margin) // 4, LANES), f32),
            short_scratch(taps),
            pltpu.SemaphoreType.DMA((3 * PARTS,)),
        ],
        cost_estimate=cost(2e7, 2.5e6),
        compiler_params=GRANT,
        name="columns",
    )(x, before, after, wide_taps)


def raw_rows_kernel(count, rows, cols, margin, taps, side_ref, x_ref, near_ref, far_ref, taps_ref, out_ref, first_ref, last_ref, buf, native, short, sems):
    even = side_ref[0] == 0
    near = jnp.where(even, margin + rows, 0)
    far = jnp.where(even, 0, margin + rows)
    height = LANES * rows
    pairs = []
    for n in range(count):
        part = pl.ds(n * height, height)
        for slot, source in enumerate((x_ref, near_ref, far_ref)):
            pairs.append((source.at[part], native.at[n, slot]))
    started = start_all(pairs, sems)
    for n in range(count):
        for slot, start in enumerate((margin, near, far)):
            started[3 * n + slot].wait()
            for r in range(rows):
                buf[start + r] = native[n, slot, pl.ds(r, LANES, stride=rows), :].T
        short_taps(taps_ref.at[n], short, taps)
        row_taps(buf, short, out_ref.at[n], rows, taps, 0, cols // SUB)
        first_ref[n] = out_ref[n, :, :margin, :]
        last_ref[n] = out_ref[n, :, cols - margin:, :]


def raw_rows(x, near, far, wide_taps, side, rows, cols, margin):
    count = x.shape[0] // (LANES * rows)
    taps = 2 * margin + 1
    return pl.pallas_call(
        functools.partial(raw_rows_kernel, count, rows, cols, margin, taps),
        in_specs=[SM, ANY, ANY, ANY, VM],
        out_specs=[VM] * 3,
        out_shape=[
            shape(count, rows, cols, LANES),
            shape(count, rows, margin, LANES),
            shape(count, rows, margin, LANES),
        ],
        scratch_shapes=[
            pltpu.VMEM((rows + 2 * margin, cols, LANES), f32),
            pltpu.VMEM((count, 3, LANES * rows, cols), f32),
            short_scratch(taps),
            pltpu.SemaphoreType.DMA((3 * count,)),
        ],
        cost_estimate=cost(3e7 * count, 4e6 * count),
        compiler_params=GRANT,
        name="raw_rows",
    )(side, x, near, far, wide_taps)


def rows_kernel(rows, cols, margin, taps, side_ref, x_ref, near_ref, far_ref, taps_ref, out_ref, buf, held, short, sems):
    even = side_ref[0] == 0
    near = jnp.where(even, margin + rows, 0)
    far = jnp.where(even, 0, margin + rows)
    share = cols // PARTS
    pairs = []
    for p in range(PARTS):
        part = pl.ds(p * share, share)
        for source, start in ((x_ref, margin), (near_ref, near), (far_ref, far)):
            pairs.append((source.at[:, part, :], buf.at[pl.ds(start, rows), part, :]))
    started = start_all(pairs, sems)
    short_taps(taps_ref.at[0], short, taps)
    for p in range(PARTS):
        for copy in started[3 * p:3 * p + 3]:
            copy.wait()
        row_taps(buf, short, held, rows, taps, p * share // SUB, share // SUB)
    for r in range(rows):
        out_ref[:, r * cols:(r + 1) * cols] = held[r].T


def rows_of(x, near, far, wide_taps, chunk, side, margin):
    rows, cols, _ = x.shape
    taps = 2 * margin + 1
    return pl.pallas_call(
        functools.partial(rows_kernel, rows, cols, margin, taps),
        grid=(1,),
        in_specs=[SM, ANY, ANY, ANY, pl.BlockSpec((1,) + wide_taps.shape[1:], lambda k: (chunk, 0, 0))],
        out_specs=pl.BlockSpec((LANES, rows * cols), lambda k: (0, 0)),
        out_shape=shape(LANES, rows * cols),
        scratch_shapes=[
            pltpu.VMEM((rows + 2 * margin, cols, LANES), f32),
            pltpu.VMEM((rows, cols, LANES), f32),
            short_scratch(taps),
            pltpu.SemaphoreType.DMA((3 * PARTS,)),
        ],
        cost_estimate=cost(2e7, 4e6),
        compiler_params=GRANT,
        name="rows",
    )(side, x, near, far, wide_taps)


def upper(chunks):
    return [(i, j) for i in range(chunks) for j in range(i, chunks)]


def gram_kernel(chunks, peers, me_ref, cosine_ref, *refs):
    xs, outs = refs[:chunks], refs[chunks:chunks + peers]
    start_ref, high, low, packed = refs[chunks + peers:]
    channels = chunks * LANES
    start = orthonormal_rows([cosine_ref[k:k + 1, :] for k in range(MODES)], channels)
    start_ref[...] = jnp.concatenate(start + [jnp.zeros((SUB - MODES, channels), f32)], axis=0)
    for k, x_ref in enumerate(xs):
        x = x_ref[...]
        h = x.astype(jnp.bfloat16)
        high[k * LANES:(k + 1) * LANES, :] = h
        low[k * LANES:(k + 1) * LANES, :] = (x - h.astype(f32)).astype(jnp.bfloat16)
    last = (((1,), (1,)), ((), ()))
    mixed = lax.dot_general(high[...], low[...], last, preferred_element_type=f32)
    gram = lax.dot_general(high[...], high[...], last, preferred_element_type=f32)
    for index, (i, j) in enumerate(upper(chunks)):
        a, b = slice(i * LANES, (i + 1) * LANES), slice(j * LANES, (j + 1) * LANES)
        packed[index * LANES:(index + 1) * LANES, :] = gram[a, b] + mixed[a, b] + mixed[b, a].T
    size = packed.shape[0] // peers
    for d in range(peers):
        piece = me_ref[0] ^ d
        outs[d][...] = packed[pl.ds(pl.multiple_of(piece * size, size), size), :]


def gram_pieces(xs, cosine, me, peers):
    chunks = len(xs)
    channels, pixels = chunks * LANES, xs[0].shape[1]
    height = len(upper(chunks)) * LANES
    return pl.pallas_call(
        functools.partial(gram_kernel, chunks, peers),
        in_specs=[SM, VM] + [VM] * chunks,
        out_specs=[VM] * (peers + 1),
        out_shape=[shape(height // peers, LANES)] * peers + [shape(SUB, channels)],
        scratch_shapes=[
            pltpu.VMEM((channels, pixels), jnp.bfloat16),
            pltpu.VMEM((channels, pixels), jnp.bfloat16),
            pltpu.VMEM((height, LANES), f32),
        ],
        cost_estimate=cost(4e9, 5e6),
        compiler_params=GRANT,
        name="gram",
    )(me, cosine, *xs)


def split_kernel(count, peers, me_ref, *refs):
    parts, outs = refs[:count], refs[count:count + peers]
    held, total, sems = refs[count + peers:]
    for copy in start_all([(part, held.at[n]) for n, part in enumerate(parts)], sems):
        copy.wait()
    value = held[0]
    for n in range(1, count):
        value = value + held[n]
    total[...] = value
    size = total.shape[0] // peers
    for d in range(peers):
        piece = me_ref[0] ^ d
        outs[d][...] = total[pl.ds(pl.multiple_of(piece * size, size), size), :]


def sum_and_split(parts, me, peers):
    height, width = parts[0].shape
    return pl.pallas_call(
        functools.partial(split_kernel, len(parts), peers),
        in_specs=[SM] + [ANY] * len(parts),
        out_specs=[VM] * peers,
        out_shape=[shape(height // peers, width)] * peers,
        scratch_shapes=[
            pltpu.VMEM((len(parts), height, width), f32),
            pltpu.VMEM((height, width), f32),
            pltpu.SemaphoreType.DMA((len(parts),)),
        ],
        compiler_params=GRANT,
        name="sum_and_split",
    )(me, *parts)


def place(pieces, target, me, sems):
    size = target.shape[0] // len(pieces)
    pairs = []
    for d, piece in enumerate(pieces):
        pairs.append((piece, target.at[pl.ds(pl.multiple_of((me ^ d) * size, size), size)]))
    return start_all(pairs, sems)


def join_kernel(peers, me_ref, *refs):
    for copy in place(refs[:peers], refs[peers], me_ref[0], refs[peers + 1]):
        copy.wait()


def join(parts, me):
    peers = len(parts)
    height, width = parts[0].shape
    return pl.pallas_call(
        functools.partial(join_kernel, peers),
        in_specs=[SM] + [ANY] * peers,
        out_specs=VM,
        out_shape=shape(height * peers, width),
        scratch_shapes=[pltpu.SemaphoreType.DMA((peers,))],
        compiler_params=GRANT,
        name="join",
    )(me, *parts)


def exchange(pieces, axis):
    peers = len(pieces)
    moved = [pieces[0]]
    for d in range(1, peers):
        moved.append(lax.ppermute(pieces[d], axis, [(i, i ^ d) for i in range(peers)]))
    return moved


def dot(u, v):
    return jnp.sum(u * v, axis=1, keepdims=True)


def orthonormal_rows(block, channels):
    done, cross = [], {}
    for index, vector in enumerate(block):
        for repeat in range(2):
            factors = [dot(q, vector) for q in done]
            for j in range(index):
                for i in range(j):
                    factors[j] = factors[j] - factors[i] * cross[i, j]
            for q, factor in zip(done, factors):
                vector = vector - factor * q
        scale_mean = dot(vector, vector) / channels + 1e-06
        vector = vector / jnp.sqrt(scale_mean) / jnp.sqrt(jnp.float32(channels))
        for i, q in enumerate(done):
            cross[i, index] = dot(q, vector)
        done.append(vector)
    return done


def cosine_rows(channels):
    channel_pos = jnp.arange(channels).astype(f32)
    mode_index = jnp.arange(MODES).astype(f32)
    return jnp.cos(jnp.pi * mode_index[:, None] * (channel_pos[None, :] + 0.5) / channels)


def spread(basis, wide, channels):
    for c in range(0, channels, LANES):
        tall = basis[:, c:c + LANES].T
        for k in range(MODES):
            wide[k, c:c + LANES, :] = jnp.broadcast_to(tall[:, k:k + 1], (LANES, LANES))


def project(xs, wide, part, channels):
    totals = [None] * MODES
    for c in range(0, channels, SUB):
        x = xs[c // LANES][c % LANES:c % LANES + SUB, part]
        for k in range(MODES):
            term = wide[k, c:c + SUB, :] * x
            totals[k] = term if totals[k] is None else totals[k] + term
    return [jnp.broadcast_to(jnp.sum(total, axis=0, keepdims=True), (SUB, LANES)) for total in totals]


def clean_kernel(chunks, peers, rows, cols, me_ref, start_ref, *refs):
    xs, pieces, out_ref = refs[:chunks], refs[chunks:chunks + peers], refs[chunks + peers]
    packed, gram, wide, coef, out_buf, piece_sems, out_sems = refs[chunks + peers + 1:]
    channels = chunks * LANES
    placed = place(pieces, packed, me_ref[0], piece_sems)
    for copy in placed:
        copy.wait()
    diagonal = jnp.zeros((1, LANES), f32)
    row_id = lax.broadcasted_iota(jnp.int32, (LANES, LANES), 0)
    col_id = lax.broadcasted_iota(jnp.int32, (LANES, LANES), 1)
    for index, (i, j) in enumerate(upper(chunks)):
        block = packed[index * LANES:(index + 1) * LANES, :]
        gram[i * LANES:(i + 1) * LANES, j * LANES:(j + 1) * LANES] = block
        if i != j:
            gram[j * LANES:(j + 1) * LANES, i * LANES:(i + 1) * LANES] = block.T
        else:
            diagonal = diagonal + jnp.sum(jnp.where(row_id == col_id, block, 0.0), axis=0, keepdims=True)
    scale = channels / jnp.sum(diagonal, axis=1, keepdims=True)
    def sweep(turn, basis):
        spread(basis, wide, channels)
        vectors = []
        for k in range(MODES):
            row = []
            for t in range(chunks):
                lanes = slice(t * LANES, (t + 1) * LANES)
                total = None
                for c in range(0, channels, SUB):
                    total = add_to(total, wide[k, c:c + SUB, :] * gram[c:c + SUB, lanes])
                row.append(jnp.sum(total, axis=0, keepdims=True))
            vectors.append(jnp.concatenate(row, axis=1) * scale)
        new = orthonormal_rows(vectors, channels)
        return jnp.concatenate(new + [jnp.zeros((SUB - MODES, channels), f32)], axis=0)

    spread(lax.fori_loop(0, SWEEPS, sweep, start_ref[...]), wide, channels)

    def coefficients(r, carry):
        values = project(xs, wide, pl.ds(pl.multiple_of(r * cols, cols), cols), channels)
        for k in range(MODES):
            coef[r, k] = values[k]
        return carry

    lax.fori_loop(0, rows, coefficients, 0)
    copies = []
    for n in range(chunks):
        def subtract(r, carry):
            part = pl.ds(pl.multiple_of(r * cols, cols), cols)
            factors = [coef[r, k] for k in range(MODES)]
            for c in range(n * LANES, (n + 1) * LANES, SUB):
                model = wide[0, c:c + SUB, :] * factors[0]
                for k in range(1, MODES):
                    model = model + wide[k, c:c + SUB, :] * factors[k]
                here = c - n * LANES
                out_buf[pl.ds(c * rows + r, SUB, stride=rows), :] = xs[n][here:here + SUB, part] - model
            return carry

        lax.fori_loop(0, rows, subtract, 0)
        block = pl.ds(n * LANES * rows, LANES * rows)
        copy = pltpu.make_async_copy(out_buf.at[block], out_ref.at[block], out_sems.at[n])
        copy.start()
        copies.append(copy)
    for copy in copies:
        copy.wait()


def clean(xs, pieces, me, start, rows, cols):
    chunks, channels = len(xs), len(xs) * LANES
    return pl.pallas_call(
        functools.partial(clean_kernel, chunks, len(pieces), rows, cols),
        in_specs=[SM, VM] + [VM] * chunks + [ANY] * len(pieces),
        out_specs=ANY,
        out_shape=shape(channels * rows, cols),
        scratch_shapes=[
            pltpu.VMEM((len(upper(chunks)) * LANES, LANES), f32),
            pltpu.VMEM((channels, channels), f32),
            pltpu.VMEM((MODES, channels, LANES), f32),
            pltpu.VMEM((rows, MODES, SUB, LANES), f32),
            pltpu.VMEM((channels * rows, cols), f32),
            pltpu.SemaphoreType.DMA((len(pieces),)),
            pltpu.SemaphoreType.DMA((chunks,)),
        ],
        cost_estimate=cost(4e7, 9e6),
        compiler_params=GRANT,
        name="clean",
    )(me, start, *xs, *pieces)


def per_device(sky_cube, beam_taps):
    taps = beam_taps.shape[1]
    margin = taps // 2
    channels, rows, cols = sky_cube.shape
    chunks = channels // LANES
    n_row, n_col = lax.axis_size("row"), lax.axis_size("col")
    me_row = lax.axis_index("row").astype(jnp.int32)
    me_col = lax.axis_index("col").astype(jnp.int32)
    side = jnp.reshape(me_row % 2, (1,))
    near_pairs = [(i, i ^ 1) for i in range(n_row)]
    far_pairs = [(i, ((i + 1) ^ 1) - 1) for i in range(1, n_row - 1)]
    right = [(i, i + 1) for i in range(n_col - 1)]
    left = [(j, i) for i, j in right]

    height = LANES * rows
    flat = sky_cube.reshape(channels * rows, cols)
    ahead = chunks // 2
    wide_taps = padded_taps(beam_taps, chunks)
    cosine = cosine_rows(channels)

    head, body = lax.optimization_barrier((flat[:ahead * height], flat))
    far_head = lax.ppermute(head, "row", far_pairs)
    near_head = lax.ppermute(head, "row", near_pairs)
    raw, first, last = prep(body, rows, cols, margin, ahead, chunks - ahead)
    before = lax.ppermute(last, "col", right)
    after = lax.ppermute(first, "col", left)
    raw, wide_taps, cosine = lax.optimization_barrier((raw, wide_taps, cosine))
    xs = [None] * chunks
    smooth, near, far = [None] * chunks, [None] * chunks, [None] * chunks
    for k in range(ahead, chunks):
        smooth[k] = columns(k - ahead, raw, before, after, wide_taps, k, margin, False)
        far[k] = lax.ppermute(smooth[k], "row", far_pairs)
        near[k] = lax.ppermute(smooth[k], "row", near_pairs)
    mixed, first_head, last_head = raw_rows(head, near_head, far_head, wide_taps, side, rows, cols, margin)
    before_head = lax.ppermute(last_head, "col", right)
    after_head = lax.ppermute(first_head, "col", left)
    for k in range(ahead, chunks):
        xs[k] = rows_of(smooth[k], near[k], far[k], wide_taps, k, side, margin)
    for k in range(ahead):
        xs[k] = columns(k, mixed, before_head, after_head, wide_taps, k, margin, True)

    row_ref, col_ref = jnp.reshape(me_row, (1,)), jnp.reshape(me_col, (1,))
    *pieces, start = gram_pieces(xs, cosine, row_ref, n_row)
    pieces = exchange(pieces, "row")
    if pieces[0].shape[0] % (SUB * n_col) == 0:
        small = exchange(sum_and_split(pieces, col_ref, n_col), "col")
        mine = functools.reduce(jnp.add, small)
        block = join(exchange([mine] * n_col, "col"), col_ref)
    else:
        mine = functools.reduce(jnp.add, pieces)
        block = functools.reduce(jnp.add, exchange([mine] * n_col, "col"))
    out = clean(xs, exchange([block] * n_row, "row"), row_ref, start, rows, cols)
    return out.reshape(channels, rows, cols)


def solution(mesh):
    placed = (P(None, ("patch", "row"), "col"), P())
    return jax.shard_map(
        per_device,
        mesh=mesh,
        in_specs=placed,
        out_specs=P(None, ("patch", "row"), "col"),
        check_vma=False,
    )
```
